1024 devices in a mesh: energy: 64 (over z, core), momentum: 16 (over y, x).
Axes of the slice: x: 4, y: 4, z: 32, core: 2. Of those that a mesh axis runs over, the one named last changes fastest.
Arguments:
- green: bfloat16 [192, 16, 2, 384, 384], P('energy', 'momentum'), may hold values from -0.3125 to 0.3125
- contact: bfloat16 [192, 16, 2, 3, 128, 128], P('energy', 'momentum'), may hold values from -6 to 6
- tile_count: int32 [192], P('energy'), may hold values from 1 to 3
- offsets: int32 [3], replicated, may hold values from 1 to 3, as said below
- pair_index: int32 [3, 16, 16], replicated, may hold values from 0 to 15
- coupling_table: float32 [3, 16], replicated, may hold values from 0.05 to 0.3
Outputs:
- lesser_tiles: bfloat16 [192, 16, 2, 3, 128, 128], P('energy', 'momentum')
- self_energy: bfloat16 [192, 16, 2, 3, 128, 128], P('energy', 'momentum')
The draws below stay inside these ranges and needn't reach their ends.
Inputs may be any that keep to these rules, and one draw needn't show every extreme that they name: `offsets`: the largest offset equals 3 in every draw.
All inputs are finite; a program needn't handle non-finite values.
Results may differ from the reference program's by a relative error of at most 0.009.
Values may be sent and summed in bfloat16 or wider, within the bound.
No kernel may reach another device: no remote copies, remote signals or barrier semaphores. Data moves between devices by JAX's collectives and lax.ppermute only.
A program may use at most 64 MiB of HBM per device.

```python
import math
import jax
import jax.numpy as jnp
from jax import lax

TILE = 128
NT = 3
B = 384
OMAX = 3
NMODE = 3
NC = 16
ITERS = 2
NE = 192
NK = 16


def draw_offsets(key, part):
    first, second = jax.random.split(jax.random.fold_in(key, 17))
    values = jax.random.randint(first, (NMODE,), 1, OMAX + 1).astype(jnp.int32)
    where = jax.random.randint(second, (), 0, NMODE).astype(jnp.int32)
    modes = jnp.arange(NMODE, dtype=jnp.int32)
    return jnp.where(modes == where, jnp.int32(OMAX), values).astype(jnp.int32)


def place_ends(entries, stream_key, smallest, top_value):
    index_at = [jax.random.randint(jax.random.fold_in(stream_key, axis), (), 0, length) for axis, length in enumerate(entries.shape)]
    widest = entries.shape.index(max(entries.shape))
    neighbour = index_at[:widest] + [(index_at[widest] + 1) % entries.shape[widest]] + index_at[widest + 1:]
    return entries.at[tuple(index_at)].set(smallest).at[tuple(neighbour)].set(top_value)


def level_of(own_key, dims, shards, low, top_value):
    def one(axis_at, shards_of):
        heights = jax.random.uniform(jax.random.fold_in(jax.random.fold_in(own_key, 6), axis_at), (shards_of,), jnp.float32, low / len(shards), top_value / len(shards))
        return jnp.repeat(jnp.exp(heights), dims[axis_at] // shards_of).reshape((-1,) + (1,) * (len(dims) - axis_at - 1))

    gain = one(*shards[0])
    for cut in shards[1:]:
        gain = gain * one(*cut)
    return gain


def noise(stream_key, shape, spread, reach, pieces=(), kind=jnp.bfloat16):
    result = jax.random.normal(stream_key, shape, jnp.float32) * spread
    if len(pieces) > 0:
        result = level_of(stream_key, shape, pieces, -0.22, 0.18) * result
    return jnp.clip(result, min=-reach, max=reach).astype(kind)


def setup_inputs(seed: int = 0) -> dict:
    keys = jax.random.split(jax.random.key(seed), 7)
    return {
        "green": noise(keys[0], (NE, NK, 2, B, B), B ** -0.5, 0.3125, ((0, 64), (1, 16))),
        "contact": noise(keys[1], (NE, NK, 2, NT, TILE, TILE), 1.0, 6.0, ((0, 64), (1, 16))),
        "tile_count": place_ends(jax.random.randint(keys[2], (NE,), 1, NT + 1), jax.random.fold_in(keys[2], 1), 1, NT).astype(jnp.int32),
        "offsets": draw_offsets(jax.random.fold_in(keys[6], 71), 0),
        "pair_index": place_ends(jax.random.randint(keys[4], (NMODE, NK, NK), 0, NC), jax.random.fold_in(keys[4], 1), 0, NC - 1).astype(jnp.int32),
        "coupling_table": jnp.clip(jnp.exp(jax.random.uniform(keys[5], (NMODE, NC), jnp.float32, math.log(0.05), math.log(0.3))), 0.05, 0.3),
    }


def couplings(pair_index, coupling_table):
    hits = (pair_index[..., None] == jnp.arange(NC, dtype=jnp.int32)).astype(jnp.float32)
    return jnp.einsum("mkqc,mc->mkq", hits, coupling_table, precision=lax.Precision.HIGHEST)


def lesser_point(block, sigma, count):
    g_real = block[0].reshape(B, NT, TILE).astype(jnp.float32)
    g_imag = block[1].reshape(B, NT, TILE).astype(jnp.float32)
    s_real = sigma[0].astype(jnp.float32)
    s_imag = sigma[1].astype(jnp.float32)
    polarization_real = jnp.einsum("rtc,tcd->rtd", g_real, s_real) - jnp.einsum("rtc,tcd->rtd", g_imag, s_imag)
    polarization_imag = jnp.einsum("rtc,tcd->rtd", g_real, s_imag) + jnp.einsum("rtc,tcd->rtd", g_imag, s_real)
    polarization_real = polarization_real.astype(jnp.bfloat16).astype(jnp.float32).reshape(NT, TILE, B)
    polarization_imag = polarization_imag.astype(jnp.bfloat16).astype(jnp.float32).reshape(NT, TILE, B)
    hamiltonian_real = block[0].astype(jnp.float32).reshape(NT, TILE, B)
    hamiltonian_imag = block[1].astype(jnp.float32).reshape(NT, TILE, B)
    phonon_propagator_real = jnp.einsum("neg,nig->nei", polarization_real, hamiltonian_real) + jnp.einsum("neg,nig->nei", polarization_imag, hamiltonian_imag)
    phonon_propagator_imag = jnp.einsum("neg,nig->nei", polarization_imag, hamiltonian_real) - jnp.einsum("neg,nig->nei", polarization_real, hamiltonian_imag)
    live = (jnp.arange(NT, dtype=jnp.int32) < count).astype(jnp.float32)[:, None, None]
    return jnp.stack([phonon_propagator_real * live, phonon_propagator_imag * live]).astype(jnp.bfloat16)


def reference(green, contact, tile_count, offsets, pair_index, coupling_table):
    coupling = couplings(pair_index, coupling_table)
    sigma = contact
    lesser = contact
    for sweep in range(ITERS):
        def one_energy(items):
            blocks, sigmas, count = items
            return jax.vmap(lambda blk, sig: lesser_point(blk, sig, count))(blocks, sigmas)
        lesser = lax.map(one_energy, (green, sigma, tile_count))
        wide = lesser.astype(jnp.float32)
        total = contact.astype(jnp.float32)
        for phonon_mode in range(NMODE):
            mixed = jnp.einsum("kq,eqabcd->ekabcd", coupling[phonon_mode], wide, precision=lax.Precision.HIGHEST)
            padded = jnp.pad(mixed, ((OMAX, OMAX), (0, 0), (0, 0), (0, 0), (0, 0), (0, 0)))
            shift = offsets[phonon_mode].astype(jnp.int32)
            lower = lax.dynamic_slice_in_dim(padded, (OMAX - shift).astype(jnp.int32), NE, 0)
            upper = lax.dynamic_slice_in_dim(padded, (OMAX + shift).astype(jnp.int32), NE, 0)
            total = total + (lower + upper)
        sigma = total.astype(jnp.bfloat16)
    return lesser, sigma
```

```python
import functools

import jax
import jax.numpy as jnp
from jax import lax
from jax.experimental import pallas as pl
from jax.experimental.pallas import tpu as pltpu
from jax.sharding import PartitionSpec as P

ITERS = 2
F32 = jnp.float32
BF16 = jnp.bfloat16
PARAMS = pltpu.CompilerParams(vmem_limit_bytes=12 << 20)
LESSER_COST = pl.CostEstimate(flops=900_000_000, bytes_accessed=4_000_000, transcendentals=0)


def coupling_kernel(span, odd, offsets, table, pairs, out):
    modes, momenta = pairs.shape[0], pairs.shape[1]
    window = 3 * span
    order = lax.broadcasted_iota(jnp.int32, (momenta, window * momenta), 0)
    column = lax.broadcasted_iota(jnp.int32, (momenta, window * momenta), 1)
    energy = lax.div(column, momenta)
    mirrored = energy + jnp.where(energy < span, 2 * span, jnp.where(energy < 2 * span, 0, -2 * span))
    energy = jnp.where(odd[0] == 1, mirrored, energy)
    spread = (lax.rem(column, momenta) == order).astype(F32)
    wide = []
    for m in range(modes):
        entry = pairs[m]
        value = jnp.zeros(entry.shape, F32)
        for c in range(table.shape[1]):
            value = jnp.where(entry == c, table[m, c], value)
        wide.append(jnp.dot(value, spread, precision=lax.Precision.HIGHEST, preferred_element_type=F32))
    for j in range(span):
        total = jnp.zeros(energy.shape, F32)
        for m in range(modes):
            low = (energy == j + span - offsets[m]).astype(F32)
            high = (energy == j + span + offsets[m]).astype(F32)
            total = total + wide[m] * (low + high)
        first = total.astype(BF16)
        out[pl.ds(j * momenta, momenta), :] = first
        out[pl.ds((span + j) * momenta, momenta), :] = (total - first.astype(F32)).astype(BF16)


def lesser_point(green, sigma, count):
    tiles, width = sigma.shape[1], sigma.shape[2]
    g_real, g_imag = green[0], green[1]
    cols = [slice(t * width, (t + 1) * width) for t in range(tiles)]
    product = []
    for t in range(tiles):
        left = jnp.concatenate([g_real[:, cols[t]], g_imag[:, cols[t]]], axis=1)
        s_real, s_imag = sigma[0, t], sigma[1, t]
        right = jnp.concatenate(
            [jnp.concatenate([s_real, s_imag], axis=1), jnp.concatenate([-s_imag, s_real], axis=1)], axis=0
        )
        product.append(jnp.dot(left, right, preferred_element_type=F32).astype(BF16))
    reals, imags = [], []
    for t in range(tiles):
        left = jnp.concatenate([product[u][cols[t]] for u in range(tiles)], axis=1)
        r = [g_real[cols[t], cols[u]] for u in range(tiles)]
        i = [g_imag[cols[t], cols[u]] for u in range(tiles)]
        top = jnp.concatenate([x for u in range(tiles) for x in (r[u], i[u])], axis=1)
        low = jnp.concatenate([x for u in range(tiles) for x in (-i[u], r[u])], axis=1)
        right = jnp.concatenate([top, low], axis=0)
        both = lax.dot_general(left, right, (((1,), (1,)), ((), ())), preferred_element_type=F32)
        live = jnp.where(t < count, 1.0, 0.0).astype(F32)
        both = (both * live).astype(BF16)
        reals.append(both[:, :width])
        imags.append(both[:, width:])
    return jnp.concatenate(reals + imags, axis=0)


def first_kernel(counts, green, contact, sent, blocks, tiles, live, sems):
    energies = green.shape[0]
    count_copy = pltpu.make_async_copy(counts, live, sems.at[2 * energies])
    copies = []
    for e in range(energies):
        copies.append(pltpu.make_async_copy(contact.at[e, 0], tiles.at[e], sems.at[2 * e]))
        copies.append(pltpu.make_async_copy(green.at[e, 0], blocks.at[e], sems.at[2 * e + 1]))
        copies[-2].start()
        copies[-1].start()
        if e == 0:
            count_copy.start()
    for e in range(energies):
        copies[2 * e].wait()
        copies[2 * e + 1].wait()
        if e == 0:
            count_copy.wait()
        flat = lesser_point(blocks[e], tiles[e], live[e])
        sent[:, e] = flat.reshape(sent.shape[0], sent.shape[2], sent.shape[3])


def next_kernel(counts, green, contact, phonon, sent, kept):
    for e in range(green.shape[0]):
        back = phonon[:, e].reshape(contact.shape[2:])
        sigma = (contact[e, 0].astype(F32) + back.astype(F32)).astype(BF16)
        flat = lesser_point(green[e, 0], sigma, counts[e])
        sent[:, e] = flat.reshape(sent.shape[0], sent.shape[2], sent.shape[3])
        kept[e, 0] = flat.reshape(kept.shape[2:])


def mix_kernel(span, matrix, across, own, beside, out, turned, mixed):
    momenta, rows = own.shape[0], own.shape[2]
    for part, source in enumerate((across, own, beside)):
        for i in range(span):
            at = (part * span + i) * momenta
            turned[:, at : at + momenta, :] = jnp.swapaxes(source[:, i], 0, 1)
    half = span * momenta
    for r in range(0, rows, 2):
        right = jnp.concatenate([turned[r], turned[r + 1]], axis=1)
        both = jnp.dot(matrix[...], right, preferred_element_type=F32)
        both = (both[:half] + both[half:]).astype(BF16)
        mixed[r] = both[:, : right.shape[1] // 2]
        mixed[r + 1] = both[:, right.shape[1] // 2 :]
    for j in range(span):
        out[:, j] = jnp.swapaxes(mixed[:, j * momenta : (j + 1) * momenta, :], 0, 1)


def total_kernel(contact, phonon, out):
    for e in range(contact.shape[0]):
        back = phonon[:, e].reshape(contact.shape[2:])
        out[e, 0] = (contact[e, 0].astype(F32) + back.astype(F32)).astype(BF16)


def couplings(span, odd, offsets, table, pairs):
    momenta = pairs.shape[1]
    smem = pl.BlockSpec(memory_space=pltpu.SMEM)
    vmem = pl.BlockSpec(memory_space=pltpu.VMEM)
    return pl.pallas_call(
        functools.partial(coupling_kernel, span),
        out_shape=jax.ShapeDtypeStruct((2 * span * momenta, 3 * span * momenta), BF16),
        in_specs=[smem, smem, smem, vmem],
        out_specs=vmem,
        name="couplings",
        compiler_params=PARAMS,
        cost_estimate=pl.CostEstimate(flops=200000, bytes_accessed=40000, transcendentals=0),
    )(odd, offsets, table, pairs)


def chunks_of(contact, momenta):
    energies, _, parts, tiles, width, _ = contact.shape
    return jax.ShapeDtypeStruct((momenta, energies, parts * tiles * width // momenta, width), BF16)


def first_lesser(counts, green, contact, momenta):
    hbm = pl.BlockSpec(memory_space=pltpu.HBM)
    energies = green.shape[0]
    return pl.pallas_call(
        first_kernel,
        out_shape=chunks_of(contact, momenta),
        in_specs=[hbm, hbm, hbm],
        out_specs=pl.BlockSpec(memory_space=pltpu.VMEM),
        scratch_shapes=[
            pltpu.VMEM((energies,) + green.shape[2:], BF16),
            pltpu.VMEM((energies,) + contact.shape[2:], BF16),
            pltpu.SMEM((energies,), jnp.int32),
            pltpu.SemaphoreType.DMA((2 * energies + 1,)),
        ],
        name="lesser_first",
        compiler_params=PARAMS,
        cost_estimate=LESSER_COST,
    )(counts, green, contact)


def next_lesser(counts, green, contact, phonon, momenta):
    vmem = pl.BlockSpec(memory_space=pltpu.VMEM)
    return pl.pallas_call(
        next_kernel,
        out_shape=(chunks_of(contact, momenta), jax.ShapeDtypeStruct(contact.shape, BF16)),
        in_specs=[pl.BlockSpec(memory_space=pltpu.SMEM), vmem, vmem, vmem],
        out_specs=(vmem, vmem),
        name="lesser_next",
        compiler_params=PARAMS,
        cost_estimate=LESSER_COST,
    )(counts, green, contact, phonon)


def mix(matrix, across, own, beside):
    momenta, span, rows, width = own.shape
    vmem = pl.BlockSpec(memory_space=pltpu.VMEM)
    return pl.pallas_call(
        functools.partial(mix_kernel, span),
        out_shape=jax.ShapeDtypeStruct(own.shape, BF16),
        in_specs=[vmem] * 4,
        out_specs=vmem,
        scratch_shapes=[
            pltpu.VMEM((rows, 3 * span * momenta, width), BF16),
            pltpu.VMEM((rows, span * momenta, width), BF16),
        ],
        name="mix",
        compiler_params=PARAMS,
        cost_estimate=pl.CostEstimate(flops=200_000_000, bytes_accessed=2_400_000, transcendentals=0),
    )(matrix, across, own, beside)


def total(contact, phonon):
    vmem = pl.BlockSpec(memory_space=pltpu.VMEM)
    return pl.pallas_call(
        total_kernel,
        out_shape=jax.ShapeDtypeStruct(contact.shape, BF16),
        in_specs=[vmem, vmem],
        out_specs=vmem,
        name="total",
        compiler_params=PARAMS,
    )(contact, phonon)


def exchange(block):
    return lax.all_to_all(block, "momentum", split_axis=0, concat_axis=0, tiled=True)


def body(green, contact, tile_count, offsets, pair_index, coupling_table):
    momenta = pair_index.shape[1]
    span = green.shape[0]
    count = lax.axis_size("energy")
    even = [(a, b) for i in range(0, count - 1, 2) for a, b in ((i, i + 1), (i + 1, i))]
    odd = [(a, b) for i in range(1, count - 1, 2) for a, b in ((i, i + 1), (i + 1, i))]
    parity = lax.rem(lax.axis_index("energy"), 2).astype(jnp.int32).reshape(1)
    matrix = couplings(span, parity, offsets, coupling_table, pair_index)
    held = [pltpu.with_memory_space_constraint(x, pltpu.HBM) for x in (tile_count, green, contact)]
    sent = first_lesser(*held, momenta)
    for sweep in range(ITERS):
        if sweep > 0:
            sent, kept = next_lesser(tile_count, green, contact, phonon, momenta)
        own = exchange(sent)
        across = lax.ppermute(own, "energy", odd)
        beside = lax.ppermute(own, "energy", even)
        phonon = exchange(mix(matrix, across, own, beside))
    return kept, total(contact, phonon)


def solution(mesh):
    in_specs = (
        P("energy", "momentum", None, None, None),
        P("energy", "momentum", None, None, None, None),
        P("energy"),
        P(),
        P(),
        P(),
    )
    out_specs = (
        P("energy", "momentum", None, None, None, None),
        P("energy", "momentum", None, None, None, None),
    )
    return jax.shard_map(body, mesh=mesh, in_specs=in_specs, out_specs=out_specs, check_vma=False)
```

```python
import functools

import jax
import jax.numpy as jnp
from jax import lax
from jax.experimental import pallas as pl
from jax.experimental.pallas import tpu as pltpu
from jax.sharding import PartitionSpec as P


ITERS = 2
F32 = jnp.float32
BF16 = jnp.bfloat16
PARAMS = pltpu.CompilerParams(vmem_limit_bytes=12 << 20)
LESSER_COST = pl.CostEstimate(flops=900_000_000, bytes_accessed=4_000_000, transcendentals=0)


def coupling_kernel(span, odd, offsets, table, pairs, out):
    modes, momenta = pairs.shape[0], pairs.shape[1]
    order = lax.broadcasted_iota(jnp.int32, (momenta, 3 * span * momenta), 0)
    column = lax.broadcasted_iota(jnp.int32, (momenta, 3 * span * momenta), 1)
    third = lax.div(column, span * momenta)
    inside = lax.rem(lax.div(column, momenta), span)
    below = jnp.where(odd[0] == 1, 1, 2)
    energy = inside + jnp.where(third == 0, span, jnp.where(third == below, 0, 2 * span))
    spread = (lax.rem(column, momenta) == order).astype(F32)
    wide = []
    for m in range(modes):
        entry = pairs[m]
        value = jnp.zeros(entry.shape, F32)
        for c in range(table.shape[1]):
            value = jnp.where(entry == c, table[m, c], value)
        wide.append(jnp.dot(value, spread, precision=lax.Precision.HIGHEST, preferred_element_type=F32))
    for j in range(span):
        total = jnp.zeros(energy.shape, F32)
        for m in range(modes):
            low = (energy == j + span - offsets[m]).astype(F32)
            high = (energy == j + span + offsets[m]).astype(F32)
            total = total + wide[m] * (low + high)
        first = total.astype(BF16)
        out[pl.ds(j * momenta, momenta), :] = first
        out[pl.ds((span + j) * momenta, momenta), :] = (total - first.astype(F32)).astype(BF16)


def lesser_point(green, sigma, count):
    tiles, width = sigma.shape[1], sigma.shape[2]
    g_real, g_imag = green[0], green[1]
    cols = [slice(t * width, (t + 1) * width) for t in range(tiles)]
    product = []
    for t in range(tiles):
        left = jnp.concatenate([g_real[:, cols[t]], g_imag[:, cols[t]]], axis=1)
        s_real, s_imag = sigma[0, t], sigma[1, t]
        right = jnp.concatenate(
            [jnp.concatenate([s_real, s_imag], axis=1), jnp.concatenate([-s_imag, s_real], axis=1)], axis=0
        )
        product.append(jnp.dot(left, right, preferred_element_type=F32).astype(BF16))
    reals, imags = [], []
    for t in range(tiles):
        left = jnp.concatenate([product[u][cols[t]] for u in range(tiles)], axis=1)
        r = [g_real[cols[t], cols[u]] for u in range(tiles)]
        i = [g_imag[cols[t], cols[u]] for u in range(tiles)]
        top = jnp.concatenate([x for u in range(tiles) for x in (r[u], i[u])], axis=1)
        low = jnp.concatenate([x for u in range(tiles) for x in (-i[u], r[u])], axis=1)
        right = jnp.concatenate([top, low], axis=0)
        both = lax.dot_general(left, right, (((1,), (1,)), ((), ())), preferred_element_type=F32)
        live = jnp.where(t < count, 1.0, 0.0).astype(F32)
        both = (both * live).astype(BF16)
        reals.append(both[:, :width])
        imags.append(both[:, width:])
    return jnp.concatenate(reals + imags, axis=0)


def first_kernel(counts, green, contact, sent, blocks, tiles, live, sems):
    energies = green.shape[0]
    count_copy = pltpu.make_async_copy(counts, live, sems.at[2 * energies])
    copies = []
    for e in range(energies):
        copies.append(pltpu.make_async_copy(contact.at[e, 0], tiles.at[e], sems.at[2 * e]))
        copies.append(pltpu.make_async_copy(green.at[e, 0], blocks.at[e], sems.at[2 * e + 1]))
        copies[-2].start()
        copies[-1].start()
        if e == 0:
            count_copy.start()
    for e in range(energies):
        copies[2 * e].wait()
        copies[2 * e + 1].wait()
        if e == 0:
            count_copy.wait()
        flat = lesser_point(blocks[e], tiles[e], live[e])
        sent[:, e] = flat.reshape(sent.shape[0], sent.shape[2], sent.shape[3])


def next_kernel(counts, green, contact, phonon, sent):
    for e in range(green.shape[0]):
        back = phonon[:, e].reshape(contact.shape[2:])
        sigma = (contact[e, 0].astype(F32) + back.astype(F32)).astype(BF16)
        flat = lesser_point(green[e, 0], sigma, counts[e])
        sent[:, e] = flat.reshape(sent.shape[0], sent.shape[2], sent.shape[3])


def turn(source, turned, start):
    momenta, span = source.shape[0], source.shape[1]
    for i in range(span):
        at = start + i * momenta
        turned[:, at : at + momenta, :] = jnp.swapaxes(source[:, i], 0, 1)


def turn_kernel(own, beside, turned):
    turn(own, turned, 0)
    turn(beside, turned, own.shape[0] * own.shape[1])


def turn_keep_kernel(own, beside, sent, turned, kept, sems):
    copies = []
    for e in range(sent.shape[1]):
        copies.append(pltpu.make_async_copy(sent.at[:, e], kept.at[e], sems.at[e]))
        copies[-1].start()
    turn_kernel(own, beside, turned)
    for copy in copies:
        copy.wait()


def mix_kernel(matrix, near, across, out, far, mixed):
    momenta, span, rows = across.shape[0], across.shape[1], across.shape[2]
    turn(across, far, 0)
    half = span * momenta
    for r in range(0, rows, 2):
        right = jnp.concatenate(
            [jnp.concatenate([near[r], far[r]], axis=0), jnp.concatenate([near[r + 1], far[r + 1]], axis=0)], axis=1
        )
        both = jnp.dot(matrix[...], right, preferred_element_type=F32)
        both = (both[:half] + both[half:]).astype(BF16)
        mixed[r] = both[:, : right.shape[1] // 2]
        mixed[r + 1] = both[:, right.shape[1] // 2 :]
    for j in range(span):
        out[:, j] = jnp.swapaxes(mixed[:, j * momenta : (j + 1) * momenta, :], 0, 1)


def total_kernel(contact, phonon, out, summed, sems):
    copies = []
    for e in range(contact.shape[0]):
        back = phonon[:, e].reshape(contact.shape[2:])
        summed[e, 0] = (contact[e, 0].astype(F32) + back.astype(F32)).astype(BF16)
        copies.append(pltpu.make_async_copy(summed.at[e], out.at[e], sems.at[e]))
        copies[-1].start()
    for copy in copies:
        copy.wait()


def couplings(span, odd, offsets, table, pairs):
    momenta = pairs.shape[1]
    smem = pl.BlockSpec(memory_space=pltpu.SMEM)
    vmem = pl.BlockSpec(memory_space=pltpu.VMEM)
    return pl.pallas_call(
        functools.partial(coupling_kernel, span),
        out_shape=jax.ShapeDtypeStruct((2 * span * momenta, 3 * span * momenta), BF16),
        in_specs=[smem, smem, smem, vmem],
        out_specs=vmem,
        name="couplings",
        compiler_params=PARAMS,
        cost_estimate=pl.CostEstimate(flops=200000, bytes_accessed=40000, transcendentals=0),
    )(odd, offsets, table, pairs)


def chunks_of(contact, momenta):
    energies, _, parts, tiles, width, _ = contact.shape
    return jax.ShapeDtypeStruct((momenta, energies, parts * tiles * width // momenta, width), BF16)


def first_lesser(counts, green, contact, momenta):
    hbm = pl.BlockSpec(memory_space=pltpu.HBM)
    energies = green.shape[0]
    return pl.pallas_call(
        first_kernel,
        out_shape=chunks_of(contact, momenta),
        in_specs=[hbm, hbm, hbm],
        out_specs=pl.BlockSpec(memory_space=pltpu.VMEM),
        scratch_shapes=[
            pltpu.VMEM((energies,) + green.shape[2:], BF16),
            pltpu.VMEM((energies,) + contact.shape[2:], BF16),
            pltpu.SMEM((energies,), jnp.int32),
            pltpu.SemaphoreType.DMA((2 * energies + 1,)),
        ],
        name="lesser_first",
        compiler_params=PARAMS,
        cost_estimate=LESSER_COST,
    )(counts, green, contact)


def next_lesser(counts, green, contact, phonon, momenta):
    vmem = pl.BlockSpec(memory_space=pltpu.VMEM)
    return pl.pallas_call(
        next_kernel,
        out_shape=chunks_of(contact, momenta),
        in_specs=[pl.BlockSpec(memory_space=pltpu.SMEM), vmem, vmem, vmem],
        out_specs=vmem,
        name="lesser_next",
        compiler_params=PARAMS,
        cost_estimate=LESSER_COST,
    )(counts, green, contact, phonon)


def turn_near(own, beside, sent=None):
    momenta, span, rows, width = own.shape
    vmem = pl.BlockSpec(memory_space=pltpu.VMEM)
    turned = jax.ShapeDtypeStruct((rows, 2 * span * momenta, width), BF16)
    cost = pl.CostEstimate(flops=1_000_000, bytes_accessed=2_400_000, transcendentals=0)
    if sent is None:
        return pl.pallas_call(
            turn_kernel,
            out_shape=turned,
            in_specs=[vmem, vmem],
            out_specs=vmem,
            name="turn",
            compiler_params=PARAMS,
            cost_estimate=cost,
        )(own, beside)
    return pl.pallas_call(
        turn_keep_kernel,
        out_shape=(turned, jax.ShapeDtypeStruct((span, momenta, rows, width), BF16)),
        in_specs=[vmem, vmem, vmem],
        out_specs=(vmem, pl.BlockSpec(memory_space=pltpu.HBM)),
        scratch_shapes=[pltpu.SemaphoreType.DMA((span,))],
        name="turn_keep",
        compiler_params=PARAMS,
        cost_estimate=cost,
    )(own, beside, sent)


def mix(matrix, near, across):
    momenta, span, rows, width = across.shape
    vmem = pl.BlockSpec(memory_space=pltpu.VMEM)
    return pl.pallas_call(
        mix_kernel,
        out_shape=jax.ShapeDtypeStruct(across.shape, BF16),
        in_specs=[vmem] * 3,
        out_specs=vmem,
        scratch_shapes=[
            pltpu.VMEM((rows, span * momenta, width), BF16),
            pltpu.VMEM((rows, span * momenta, width), BF16),
        ],
        name="mix",
        compiler_params=PARAMS,
        cost_estimate=pl.CostEstimate(flops=200_000_000, bytes_accessed=2_400_000, transcendentals=0),
    )(matrix, near, across)


def total(contact, phonon):
    vmem = pl.BlockSpec(memory_space=pltpu.VMEM)
    return pl.pallas_call(
        total_kernel,
        out_shape=jax.ShapeDtypeStruct(contact.shape, BF16),
        in_specs=[vmem, vmem],
        out_specs=pl.BlockSpec(memory_space=pltpu.HBM),
        scratch_shapes=[pltpu.VMEM(contact.shape, BF16), pltpu.SemaphoreType.DMA((contact.shape[0],))],
        name="total",
        compiler_params=PARAMS,
    )(contact, phonon)


def exchange(block):
    return lax.all_to_all(block, "momentum", split_axis=0, concat_axis=0, tiled=True)


def body(green, contact, tile_count, offsets, pair_index, coupling_table):
    momenta = pair_index.shape[1]
    span = green.shape[0]
    count = lax.axis_size("energy")
    even = [(a, b) for i in range(0, count - 1, 2) for a, b in ((i, i + 1), (i + 1, i))]
    odd = [(a, b) for i in range(1, count - 1, 2) for a, b in ((i, i + 1), (i + 1, i))]
    parity = lax.rem(lax.axis_index("energy"), 2).astype(jnp.int32).reshape(1)
    matrix = couplings(span, parity, offsets, coupling_table, pair_index)
    held = [pltpu.with_memory_space_constraint(x, pltpu.HBM) for x in (tile_count, green, contact)]
    sent = first_lesser(*held, momenta)
    for sweep in range(ITERS):
        if sweep > 0:
            sent = next_lesser(tile_count, green, contact, phonon, momenta)
        own = exchange(sent)
        across = lax.ppermute(own, "energy", odd)
        beside = lax.ppermute(own, "energy", even)
        if sweep < ITERS - 1:
            near = turn_near(own, beside)
        else:
            near, kept = turn_near(own, beside, sent)
        phonon = exchange(mix(matrix, near, across))
    return kept.reshape(contact.shape), total(contact, phonon)


def solution(mesh):
    in_specs = (
        P("energy", "momentum", None, None, None),
        P("energy", "momentum", None, None, None, None),
        P("energy"),
        P(),
        P(),
        P(),
    )
    out_specs = (
        P("energy", "momentum", None, None, None, None),
        P("energy", "momentum", None, None, None, None),
    )
    return jax.shard_map(body, mesh=mesh, in_specs=in_specs, out_specs=out_specs, check_vma=False)
```
